32 devices in a mesh: ctx: 8 (over z, y), tp: 4 (over x, core).
Axes of the slice: x: 2, y: 2, z: 4, core: 2. Of those that a mesh axis runs over, the one named last changes fastest.
Arguments:
- features: bfloat16 [3, 1024, 4096], P(None, 'ctx', 'tp'), may hold values from -6 to 6
- out_grad: bfloat16 [1024, 4096], P('ctx', 'tp'), may hold values from -6 to 6
- attn_parts: bfloat16 [4, 1024, 4096], P('tp', 'ctx'), may hold values from -6 to 6
- short_filt: bfloat16 [3, 256, 7], P(None, 'tp'), may hold values from -2 to 2
- med_filt: bfloat16 [256, 128], P('tp'), may hold values from -0.5 to 0.5
- piece_home: int32 [32], replicated, may hold values from 0 to 7, as said below
- piece_start: int32 [32], replicated, may hold values from 0 to 96, as said below
Outputs:
- feat_grad: bfloat16 [3, 1024, 4096], P(None, 'ctx', 'tp')
- short_grad: float32 [3, 256, 7], P(None, 'tp')
- med_grad: float32 [256, 128], P('tp')
The draws below stay inside these ranges and needn't reach their ends.
Inputs may be any that keep to these rules, and one draw needn't show every extreme that they name: `piece_home`: entry i * 4 + l names the home device of the piece of 32 rows that starts at row l * 32 of device i in the balanced layout. With piece_start the entries name every piece of every home device exactly once, and no device of the balanced layout holds two pieces of the same home device. `piece_start`: A multiple of 32.
All inputs are finite; a program needn't handle non-finite values.
Results may differ from the reference program's by a relative error of at most 0.012.
Values may be sent and summed in bfloat16 or wider, within the bound.
A program may use at most 64 MiB of HBM per device.

```python
import math
import jax
import jax.numpy as jnp
from jax import lax

CH = 4096
GROUP = 16
SK = 7
MK = 128
TOK_DEV = 128
PIECES_DEV = 4
PIECE = 32
TOKENS = 1024
GROUPS = 256
N_CTX = 8
N_TP = 4


def route_tables(key):
    base = jax.random.fold_in(key, 7)
    keys = jax.random.split(base, 5)
    offsets = jax.random.permutation(keys[0], N_CTX)[:PIECES_DEV]
    outer = jax.random.permutation(keys[1], N_CTX)
    inner = jax.random.permutation(keys[2], N_CTX)
    local = jax.vmap(lambda one: jax.random.permutation(one, PIECES_DEV))(jax.random.split(keys[3], N_CTX))
    slots = jax.vmap(lambda one: jax.random.permutation(one, PIECES_DEV))(jax.random.split(keys[4], N_CTX))
    home = outer[(inner[:, None] + offsets[local]) % N_CTX]
    start = PIECE * slots[home, local]
    return (home.reshape(-1).astype(jnp.int32), start.reshape(-1).astype(jnp.int32))


def draw_piece_home(key, part):
    return route_tables(key)[0]


def draw_piece_start(key, part):
    return route_tables(key)[1]


def raised(array, key, source, target, blocks, factor):
    def block_of(dim):
        return (jnp.arange(array.shape[dim]) // (array.shape[dim] // blocks)).reshape((-1,) + (1,) * (array.ndim - 1 - dim))

    near = jax.random.permutation(key, blocks)[block_of(target)]
    far = (block_of(target) + blocks // 2) % blocks
    return jnp.where((block_of(source) == near) | (block_of(source) == far), factor * array, array)


def level_of(key, extent, pieces, smallest, high):
    def one(axis_at, parts):
        draws = jax.random.uniform(jax.random.fold_in(jax.random.fold_in(key, 6), axis_at), (parts,), jnp.float32, smallest / len(pieces), high / len(pieces))
        return jnp.repeat(jnp.exp(draws), extent[axis_at] // parts).reshape((-1,) + (1,) * (len(extent) - axis_at - 1))

    factor_of = one(*pieces[0])
    for cut in pieces[1:]:
        factor_of = factor_of * one(*cut)
    return factor_of


def bell_draw(key, shape, deviation, limit, shards=(), kind=jnp.bfloat16):
    result = deviation * jax.random.normal(key, shape, jnp.float32)
    if shards:
        result = result * level_of(key, shape, shards, -0.22, 0.18)
    return jnp.clip(result, -limit, limit).astype(kind)


def gaussian_with(stream_key, extent, scale, most, shards, heavy, kind=jnp.bfloat16):
    array = scale * jax.random.normal(stream_key, extent, jnp.float32)
    if shards:
        array = array * level_of(stream_key, extent, shards, -0.22, 0.18)
    return jnp.clip(raised(array, jax.random.fold_in(stream_key, 3), *heavy), -most, most).astype(kind)


def setup_inputs(seed: int = 0) -> dict:
    key_of = jax.random.split(jax.random.key(seed), 8)
    return {
        "features": bell_draw(key_of[0], (3, TOKENS, CH), 1.0, 6.0, ((1, 8), (2, 4))),
        "out_grad": bell_draw(key_of[1], (TOKENS, CH), 1.0, 6.0, ((0, 8), (1, 4))),
        "attn_parts": gaussian_with(key_of[2], (N_TP, TOKENS, CH), 0.5, 6.0, ((0, 4), (1, 8)), (0, 2, 4, 2.0)),
        "short_filt": bell_draw(key_of[3], (3, GROUPS, SK), SK ** -0.5, 2.0, ((1, 4),)),
        "med_filt": bell_draw(key_of[4], (GROUPS, MK), MK ** -0.5, 0.5, ((0, 4),)),
        "piece_home": draw_piece_home(jax.random.fold_in(key_of[7], 71), 0),
        "piece_start": draw_piece_start(jax.random.fold_in(key_of[7], 71), 0),
    }


def causal_table(filt):
    taps = filt.shape[1]
    lag = jnp.arange(taps, dtype=jnp.int32)[:, None] + taps - 1 - jnp.arange(2 * taps - 1, dtype=jnp.int32)[None, :]
    valid = (lag >= 0) & (lag < taps)
    return jnp.where(valid[None], filt[:, jnp.clip(lag, 0, taps - 1)], jnp.float32(0.0))

def anti_table(filt):
    taps = filt.shape[1]
    lag = jnp.arange(2 * taps - 1, dtype=jnp.int32)[None, :] - jnp.arange(taps, dtype=jnp.int32)[:, None]
    valid = (lag >= 0) & (lag < taps)
    return jnp.where(valid[None], filt[:, jnp.clip(lag, 0, taps - 1)], jnp.float32(0.0))

def band_apply(table, padded, rows):
    taps = table.shape[1]
    groups = table.shape[0]
    width = padded.shape[1]

    def one(block):
        window = lax.dynamic_slice_in_dim(padded, block * taps, 2 * taps - 1, 0).astype(jnp.float32)
        window = window.reshape(2 * taps - 1, groups, width // groups)
        return jnp.einsum('gtu,ugc->tgc', table, window).reshape(taps, width)
    return lax.map(one, jnp.arange(rows // taps, dtype=jnp.int32)).reshape(rows, width)

def lag_sums(grads, padded, rows, groups):
    taps = MK
    width = grads.shape[1]
    rowsel = jnp.arange(taps, dtype=jnp.int32)[:, None]
    colsel = rowsel + taps - 1 - jnp.arange(taps, dtype=jnp.int32)[None, :]

    def one(total, block):
        left = lax.dynamic_slice_in_dim(grads, block * taps, taps, 0).astype(jnp.float32).reshape(taps, groups, width // groups)
        window = lax.dynamic_slice_in_dim(padded, block * taps, 2 * taps - 1, 0).astype(jnp.float32)
        window = window.reshape(2 * taps - 1, groups, width // groups)
        cross = jnp.einsum('tgc,ugc->gtu', left, window)
        picked = cross[:, rowsel, colsel]
        return (total + lax.optimization_barrier(jnp.sum(picked, axis=1)), None)
    start = jnp.zeros((groups, taps), jnp.float32)
    total, _ = lax.scan(one, start, jnp.arange(rows // taps, dtype=jnp.int32))
    return total

def short_forward(stream, filt):
    weights = jnp.repeat(filt, GROUP, axis=0)
    padded = jnp.pad(stream.astype(jnp.float32), ((SK - 1, 0), (0, 0)))
    total = jnp.zeros((TOKENS, stream.shape[1]), jnp.float32)
    for lag in range(SK):
        total = total + weights[:, lag][None, :] * padded[SK - 1 - lag:SK - 1 - lag + TOKENS]
    return total

def short_backward(grads, filt):
    weights = jnp.repeat(filt, GROUP, axis=0)
    padded = jnp.pad(grads, ((0, SK - 1), (0, 0)))
    total = jnp.zeros_like(grads)
    for lag in range(SK):
        total = total + weights[:, lag][None, :] * padded[lag:lag + TOKENS]
    return total

def short_lags(grads, stream):
    padded = jnp.pad(stream.astype(jnp.float32), ((SK - 1, 0), (0, 0)))
    columns = []
    for lag in range(SK):
        summed = lax.optimization_barrier(jnp.sum(grads * padded[SK - 1 - lag:SK - 1 - lag + TOKENS], axis=0))
        columns.append(summed.reshape(-1, GROUP).sum(axis=1))
    return jnp.stack(columns, axis=1)

def reference(features, out_grad, attn_parts, short_filt, med_filt, piece_home, piece_start):
    attn_sum = lax.optimization_barrier(jnp.sum(attn_parts.astype(jnp.float32), axis=0)).astype(jnp.bfloat16)
    target = (piece_home * TOK_DEV + piece_start)[:, None] + jnp.arange(PIECE, dtype=jnp.int32)[None, :]
    attn_home = jnp.zeros_like(attn_sum).at[target.reshape(-1)].set(attn_sum)
    slab = CH // N_TP
    slab_groups = slab // GROUP
    factor = 1.0 / math.sqrt(TOKENS * GROUP)
    grads_out, shorts_out, meds_out = ([], [], [])
    for index in range(N_TP):
        low = index * slab
        stream_in = features[:, :, low:low + slab]
        filt_short = short_filt[:, index * slab_groups:(index + 1) * slab_groups, :].astype(jnp.float32)
        filt_med = med_filt[index * slab_groups:(index + 1) * slab_groups, :].astype(jnp.float32)
        grad = out_grad[:, low:low + slab].astype(jnp.float32) + attn_home[:, low:low + slab].astype(jnp.float32)
        query = short_forward(stream_in[0], filt_short[0])
        keys = short_forward(stream_in[1], filt_short[1])
        values = short_forward(stream_in[2], filt_short[2])
        keyval = (keys * values).astype(jnp.bfloat16)
        key_pad = jnp.pad(keyval, ((MK - 1, 0), (0, 0)))
        mixed = band_apply(causal_table(filt_med), key_pad, TOKENS)
        dquery = grad * mixed
        dmix = (grad * query).astype(jnp.bfloat16)
        dkeyval = band_apply(anti_table(filt_med), jnp.pad(dmix, ((0, MK - 1), (0, 0))), TOKENS)
        dstreams = [dquery, dkeyval * values, dkeyval * keys]
        grads_out.append(jnp.stack([short_backward(dstreams[s], filt_short[s]) for s in range(3)]).astype(jnp.bfloat16))
        shorts_out.append(jnp.stack([short_lags(dstreams[s], stream_in[s]) for s in range(3)]) * factor)
        meds_out.append(lag_sums(dmix, key_pad, TOKENS, slab_groups) * factor)
    return (jnp.concatenate(grads_out, axis=2), jnp.concatenate(shorts_out, axis=1), jnp.concatenate(meds_out, axis=0))
```

```python
import functools
import math

import jax
import jax.numpy as jnp
from jax import lax
from jax.experimental import pallas as pl
from jax.experimental.pallas import tpu as pltpu
from jax.sharding import PartitionSpec as P

GROUP = 16
LANES = 256
PARAMS = pltpu.CompilerParams(vmem_limit_bytes=32 * 1024 * 1024)


def shifted(x, axis, by):
    size = lax.axis_size(axis)
    pairs = [(i, i + by) for i in range(size) if 0 <= i + by < size]
    return lax.ppermute(x, axis, pairs)


def cost(flops, bytes_accessed):
    return pl.CostEstimate(flops=flops, bytes_accessed=bytes_accessed, transcendentals=0)


def call(body, grid, in_specs, out_specs, out_shape, flops, moved, scratch=()):
    return pl.pallas_call(
        body,
        grid=grid,
        in_specs=in_specs,
        out_specs=out_specs,
        out_shape=out_shape,
        scratch_shapes=list(scratch),
        compiler_params=PARAMS,
        cost_estimate=cost(flops, moved),
    )


def streams_kernel(feat_ref, rim_ref, wt_ref, streams_ref, kv_ref, ext):
    rows = feat_ref.shape[1]
    taps = wt_ref.shape[1]
    found = []
    for s in range(3):
        ext[8 - taps + 1 : 8] = rim_ref[s].astype(jnp.float32)
        ext[8:] = feat_ref[s].astype(jnp.float32)
        total = wt_ref[s, 0:1, :] * ext[8:]
        for lag in range(1, taps):
            total = total + wt_ref[s, lag : lag + 1, :] * ext[8 - lag : 8 - lag + rows]
        streams_ref[s] = total
        found.append(total)
    kv_ref[...] = (found[1] * found[2]).astype(kv_ref.dtype)


def plane(rows, axis):
    return lax.broadcasted_iota(jnp.int32, (rows, rows), axis)


def mixed_kernel(filt_ref, before_ref, own_ref, mixed_ref):
    taps = filt_ref.shape[1]
    width = own_ref.shape[1]
    window = jnp.concatenate([before_ref[...], own_ref[...]], axis=0)
    t, s = plane(taps, 0), plane(taps, 1)
    owner = lax.broadcasted_iota(jnp.int32, (taps, width), 1) // GROUP
    total = jnp.zeros((taps, width), jnp.float32)
    for g in range(width // GROUP):
        line = jnp.broadcast_to(filt_ref[g : g + 1, :], (taps, taps))
        wheel = pltpu.roll(line, 0, 1, stride=1, stride_axis=0)
        table = jnp.concatenate(
            [jnp.where(s > t, wheel, 0.0), jnp.where(s <= t, wheel, 0.0)], axis=1
        ).astype(own_ref.dtype)
        product = jnp.dot(table, window, preferred_element_type=jnp.float32)
        total = jnp.where(owner == g, product, total)
    mixed_ref[...] = total


def back_kernel(
    filt_ref, dmix_ref, after_ref, kv_ref, before_ref, streams_ref, dq_ref, feat_ref, rim_ref,
    dstreams_ref, med_ref, short_ref, ext,
):
    taps = filt_ref.shape[1]
    width = dmix_ref.shape[1]
    kind = dmix_ref.dtype
    t, s = plane(taps, 0), plane(taps, 1)
    owner = lax.broadcasted_iota(jnp.int32, (taps, width), 1) // GROUP
    dmix = dmix_ref[...]
    window = jnp.concatenate([dmix, after_ref[...]], axis=0)
    flip = jnp.where(t + s == taps - 1, 1.0, 0.0).astype(kind)
    flipped = jnp.dot(flip, dmix, preferred_element_type=jnp.float32)
    keyval = jnp.concatenate([before_ref[...], kv_ref[...]], axis=0)
    total = jnp.zeros((taps, width), jnp.float32)
    for g in range(width // GROUP):
        line = jnp.broadcast_to(filt_ref[g : g + 1, :], (taps, taps))
        wheel = pltpu.roll(line, 0, 1, stride=1, stride_axis=0)
        table = jnp.concatenate(
            [jnp.where(s >= t, wheel, 0.0), jnp.where(s < t, wheel, 0.0)], axis=1
        ).astype(kind)
        product = jnp.dot(table, window, preferred_element_type=jnp.float32)
        total = jnp.where(owner == g, product, total)
        left = jnp.where(owner == g, flipped, 0.0).astype(kind)
        cross = lax.dot_general(
            left, keyval, (((1,), (1,)), ((), ())), preferred_element_type=jnp.float32
        )
        ring = jnp.where(s + t <= taps - 1, cross[:, taps:], cross[:, :taps])
        ring = pltpu.roll(ring, 0, 1, stride=1, stride_axis=0)
        med_ref[g : g + 1, :] = jnp.sum(ring, axis=0, keepdims=True)
    rows = feat_ref.shape[1]
    short_taps = short_ref.shape[1]
    parts = (dq_ref[...], total * streams_ref[1], total * streams_ref[0])
    for k in range(3):
        dstreams_ref[k] = parts[k]
        ext[8 - short_taps + 1 : 8] = rim_ref[k].astype(jnp.float32)
        ext[8:] = feat_ref[k].astype(jnp.float32)
        for lag in range(short_taps):
            short_ref[k, lag : lag + 1, :] = jnp.sum(
                parts[k] * ext[8 - lag : 8 - lag + rows], axis=0, keepdims=True
            )


def feat_kernel(ds_ref, rim_ref, wt_ref, out_ref, ext):
    rows = ds_ref.shape[1]
    taps = wt_ref.shape[1]
    for s in range(3):
        ext[0:rows] = ds_ref[s]
        ext[rows : rows + taps - 1] = rim_ref[s].astype(jnp.float32)
        total = wt_ref[s, 0:1, :] * ds_ref[s]
        for lag in range(1, taps):
            total = total + wt_ref[s, lag : lag + 1, :] * ext[lag : lag + rows]
        out_ref[s] = total.astype(out_ref.dtype)


def shards(features, out_grad, attn_parts, short_filt, med_filt, piece_home, piece_start):
    rows, width = out_grad.shape
    groups, taps = med_filt.shape
    short_taps = short_filt.shape[2]
    ctx_count = lax.axis_size("ctx")
    own_index = lax.axis_index("ctx")
    per_device = ctx_count // 2
    piece_rows = rows // per_device
    factor = 1.0 / math.sqrt(rows * ctx_count * GROUP)
    chunk = LANES if width % LANES == 0 else width
    steps = width // chunk
    grid = (steps,)
    near = chunk // GROUP

    def lead3(n):
        return pl.BlockSpec((3, n, chunk), lambda i: (0, 0, i))

    def flat(n):
        return pl.BlockSpec((n, chunk), lambda i: (0, i))

    filt_spec = pl.BlockSpec((near, taps), lambda i: (i, 0))
    f32, half = jnp.float32, features.dtype

    everyone = piece_home.reshape(ctx_count, per_device)
    positions = (piece_start // piece_rows).reshape(ctx_count, per_device)
    local_home = lax.dynamic_slice_in_dim(everyone, own_index, 1, 0)[0]
    device_ids = jnp.arange(ctx_count, dtype=jnp.int32)
    slot_ids = jnp.arange(per_device, dtype=jnp.int32)
    matches = local_home[None, :] == device_ids[:, None]
    send_slot = jnp.sum(jnp.where(matches, slot_ids[None, :], 0), axis=1)
    keyed = jnp.where(everyone == own_index, positions, -1)
    hits = jnp.any(keyed[:, :, None] == slot_ids[None, None, :], axis=1)
    source_of = jnp.sum(jnp.where(hits, device_ids[:, None], 0), axis=0)
    summed = lax.psum_scatter(attn_parts[0], "tp", scatter_dimension=1, tiled=True)
    pieces = summed.reshape(per_device, piece_rows, -1)
    attn_home = lax.all_to_all(
        pieces[send_slot], "ctx", split_axis=0, concat_axis=0, tiled=True
    )[source_of].reshape(rows, -1)

    short_weights = jnp.transpose(jnp.repeat(short_filt, GROUP, axis=1), (0, 2, 1)).astype(f32)
    filt = med_filt.astype(f32)
    filt_back = jnp.roll(filt[:, ::-1], 1, axis=1)
    stream_rim = shifted(features[:, rows - short_taps + 1 :, :], "ctx", 1)
    streams, keyval = call(
        streams_kernel,
        grid,
        [lead3(rows), lead3(short_taps - 1), lead3(short_taps)],
        (lead3(rows), flat(rows)),
        (
            jax.ShapeDtypeStruct((3, rows, width), f32),
            jax.ShapeDtypeStruct((rows, width), half),
        ),
        3 * 14 * rows * width,
        20 * rows * width,
        [pltpu.VMEM((rows + 8, chunk), f32)],
    )(features, stream_rim, short_weights)
    key_rim = shifted(keyval, "ctx", 1)
    mixed = call(
        mixed_kernel,
        grid,
        [filt_spec, flat(rows), flat(rows)],
        flat(rows),
        jax.ShapeDtypeStruct((rows, width), f32),
        4 * groups * taps * taps * chunk,
        8 * rows * width,
    )(filt_back, key_rim, keyval)

    grad = out_grad.astype(f32) + attn_home.astype(f32)
    dmix = (grad * streams[0]).astype(half)
    dquery = grad * mixed
    grad_rim = shifted(dmix, "ctx", -1)
    pair = streams[1:]
    dstreams, med_part, short_cols = call(
        back_kernel,
        grid,
        [
            filt_spec, flat(rows), flat(rows), flat(rows), flat(rows),
            pl.BlockSpec((2, rows, chunk), lambda i: (0, 0, i)),
            flat(rows), lead3(rows), lead3(short_taps - 1),
        ],
        (lead3(rows), filt_spec, lead3(short_taps)),
        (
            jax.ShapeDtypeStruct((3, rows, width), f32),
            jax.ShapeDtypeStruct((groups, taps), f32),
            jax.ShapeDtypeStruct((3, short_taps, width), f32),
        ),
        8 * groups * taps * taps * chunk,
        40 * rows * width,
        [pltpu.VMEM((rows + 8, chunk), f32)],
    )(filt, dmix, grad_rim, keyval, key_rim, pair, dquery, features, stream_rim)
    tail_rim = shifted(dstreams[:, : short_taps - 1].astype(half), "ctx", -1)
    feat_grad = call(
        feat_kernel,
        grid,
        [lead3(rows), lead3(short_taps - 1), lead3(short_taps)],
        lead3(rows),
        jax.ShapeDtypeStruct((3, rows, width), half),
        3 * 14 * rows * width,
        20 * rows * width,
        [pltpu.VMEM((rows + 8, chunk), f32)],
    )(dstreams, tail_rim, short_weights)
    member = (
        jnp.arange(width, dtype=jnp.int32)[:, None] // GROUP
        == jnp.arange(groups, dtype=jnp.int32)[None, :]
    ).astype(f32)
    short_part = jnp.einsum(
        "slw,wg->sgl", short_cols, member, precision=lax.Precision.HIGHEST
    )
    totals = lax.psum((short_part, med_part), "ctx")
    return (feat_grad, totals[0] * factor, totals[1][:, ::-1] * factor)


def solution(mesh):
    return jax.shard_map(
        shards,
        mesh=mesh,
        in_specs=(
            P(None, "ctx", "tp"),
            P("ctx", "tp"),
            P("tp", "ctx", None),
            P(None, "tp", None),
            P("tp", None),
            P(),
            P(),
        ),
        out_specs=(P(None, "ctx", "tp"), P(None, "tp", None), P("tp", None)),
        check_vma=False,
    )
```

```python
import functools
import math

import jax
import jax.numpy as jnp
from jax import lax
from jax.experimental import pallas as pl
from jax.experimental.pallas import tpu as pltpu
from jax.sharding import PartitionSpec as P

GROUP = 16
MESH = pl.DeviceIdType.MESH
LANES = 256
PARAMS = pltpu.CompilerParams(vmem_limit_bytes=32 * 1024 * 1024)


def shifted(x, axis, by):
    size = lax.axis_size(axis)
    pairs = [(i, i + by) for i in range(size) if 0 <= i + by < size]
    return lax.ppermute(x, axis, pairs)


def cost(flops, bytes_accessed):
    return pl.CostEstimate(flops=flops, bytes_accessed=bytes_accessed, transcendentals=0)


def call(body, grid, in_specs, out_specs, out_shape, flops, moved, scratch=()):
    return pl.pallas_call(
        body,
        grid=grid,
        in_specs=in_specs,
        out_specs=out_specs,
        out_shape=out_shape,
        scratch_shapes=list(scratch),
        compiler_params=PARAMS,
        cost_estimate=cost(flops, moved),
    )


def streams_kernel(feat_ref, rim_ref, wt_ref, streams_ref, kv_ref, ext):
    rows = feat_ref.shape[1]
    taps = wt_ref.shape[1]
    found = []
    for s in range(3):
        ext[8 - taps + 1 : 8] = rim_ref[s].astype(jnp.float32)
        ext[8:] = feat_ref[s].astype(jnp.float32)
        total = wt_ref[s, 0:1, :] * ext[8:]
        for lag in range(1, taps):
            total = total + wt_ref[s, lag : lag + 1, :] * ext[8 - lag : 8 - lag + rows]
        streams_ref[s] = total
        found.append(total)
    kv_ref[...] = (found[1] * found[2]).astype(kv_ref.dtype)


def plane(rows, axis):
    return lax.broadcasted_iota(jnp.int32, (rows, rows), axis)


def mixed_kernel(filt_ref, before_ref, own_ref, mixed_ref):
    taps = filt_ref.shape[1]
    width = own_ref.shape[1]
    window = jnp.concatenate([before_ref[...], own_ref[...]], axis=0)
    t, s = plane(taps, 0), plane(taps, 1)
    owner = lax.broadcasted_iota(jnp.int32, (taps, width), 1) // GROUP
    total = jnp.zeros((taps, width), jnp.float32)
    for g in range(width // GROUP):
        line = jnp.broadcast_to(filt_ref[g : g + 1, :], (taps, taps))
        wheel = pltpu.roll(line, 0, 1, stride=1, stride_axis=0)
        table = jnp.concatenate(
            [jnp.where(s > t, wheel, 0.0), jnp.where(s <= t, wheel, 0.0)], axis=1
        ).astype(own_ref.dtype)
        product = jnp.dot(table, window, preferred_element_type=jnp.float32)
        total = jnp.where(owner == g, product, total)
    mixed_ref[...] = total


def back_kernel(
    filt_ref, dmix_ref, after_ref, kv_ref, before_ref, streams_ref, dq_ref, feat_ref, rim_ref,
    dstreams_ref, med_ref, short_ref, head_ref, ext,
):
    taps = filt_ref.shape[1]
    width = dmix_ref.shape[1]
    kind = dmix_ref.dtype
    t, s = plane(taps, 0), plane(taps, 1)
    owner = lax.broadcasted_iota(jnp.int32, (taps, width), 1) // GROUP
    dmix = dmix_ref[...]
    window = jnp.concatenate([dmix, after_ref[...]], axis=0)
    flip = jnp.where(t + s == taps - 1, 1.0, 0.0).astype(kind)
    flipped = jnp.dot(flip, dmix, preferred_element_type=jnp.float32)
    keyval = jnp.concatenate([before_ref[...], kv_ref[...]], axis=0)
    total = jnp.zeros((taps, width), jnp.float32)
    for g in range(width // GROUP):
        line = jnp.broadcast_to(filt_ref[g : g + 1, :], (taps, taps))
        wheel = pltpu.roll(line, 0, 1, stride=1, stride_axis=0)
        table = jnp.concatenate(
            [jnp.where(s >= t, wheel, 0.0), jnp.where(s < t, wheel, 0.0)], axis=1
        ).astype(kind)
        product = jnp.dot(table, window, preferred_element_type=jnp.float32)
        total = jnp.where(owner == g, product, total)
        left = jnp.where(owner == g, flipped, 0.0).astype(kind)
        cross = lax.dot_general(
            left, keyval, (((1,), (1,)), ((), ())), preferred_element_type=jnp.float32
        )
        ring = jnp.where(s + t <= taps - 1, cross[:, taps:], cross[:, :taps])
        ring = pltpu.roll(ring, 0, 1, stride=1, stride_axis=0)
        med_ref[g : g + 1, :] = jnp.sum(ring, axis=0, keepdims=True)
    rows = feat_ref.shape[1]
    short_taps = short_ref.shape[1]
    parts = (dq_ref[...], total * streams_ref[1], total * streams_ref[0])
    for k in range(3):
        dstreams_ref[k] = parts[k]
        head_ref[k] = parts[k][:8].astype(head_ref.dtype)
        ext[8 - short_taps + 1 : 8] = rim_ref[k].astype(jnp.float32)
        ext[8:] = feat_ref[k].astype(jnp.float32)
        for lag in range(short_taps):
            short_ref[k, lag : lag + 1, :] = jnp.sum(
                parts[k] * ext[8 - lag : 8 - lag + rows], axis=0, keepdims=True
            )


def final_kernel(
    n, part_ref, ds_ref, head_ref, wt_ref, feat_ref, total_ref,
    landed, gathered, rim, ext, send1, recv1, send2, recv2, send_rim, recv_rim,
):
    me = lax.axis_index("ctx")
    rows, width = ds_ref.shape[1:]
    taps = wt_ref.shape[1]
    chunk = ext.shape[1]
    barrier = pltpu.get_barrier_semaphore()

    def greet(k, carry):
        pl.semaphore_signal(
            barrier, inc=1, device_id={"ctx": lax.rem(me + k, n)}, device_id_type=MESH
        )
        return carry

    lax.fori_loop(1, n, greet, 0)
    pl.semaphore_wait(barrier, n - 1)

    def scatter(k):
        peer = lax.rem(me + k, n)
        return pltpu.make_async_remote_copy(
            part_ref.at[peer], landed.at[k], send1.at[k], recv1.at[k],
            device_id={"ctx": peer}, device_id_type=MESH,
        )

    def gather(k):
        peer = lax.rem(me + k, n)
        return pltpu.make_async_remote_copy(
            gathered.at[me], gathered.at[me], send2.at[k], recv2.at[k],
            device_id={"ctx": peer}, device_id_type=MESH,
        )

    def each(copy, act):
        def step(k, carry):
            act(copy(k))
            return carry

        lax.fori_loop(1, n, step, 0)

    halo = pltpu.make_async_remote_copy(
        head_ref, rim, send_rim, recv_rim,
        device_id={"ctx": lax.rem(me + n - 1, n)}, device_id_type=MESH,
    )
    halo.start()
    each(scatter, lambda c: c.start())
    landed[0] = part_ref[me]
    each(scatter, lambda c: c.wait())
    total = landed[0]
    for k in range(1, n):
        total = total + landed[k]
    gathered[me] = total
    each(gather, lambda c: c.start())
    halo.wait()
    live = jnp.where(me == n - 1, 0.0, 1.0)
    for s in range(3):
        for c in range(width // chunk):
            cols = slice(c * chunk, (c + 1) * chunk)
            ext[0:rows] = ds_ref[s, :, cols]
            ext[rows : rows + 8] = live * rim[s, :, cols].astype(jnp.float32)
            total = wt_ref[s, 0:1, cols] * ds_ref[s, :, cols]
            for lag in range(1, taps):
                total = total + wt_ref[s, lag : lag + 1, cols] * ext[lag : lag + rows]
            feat_ref[s, :, cols] = total.astype(feat_ref.dtype)
    each(gather, lambda c: c.wait())
    total_ref[...] = gathered[...]


def shards(features, out_grad, attn_parts, short_filt, med_filt, piece_home, piece_start):
    rows, width = out_grad.shape
    groups, taps = med_filt.shape
    short_taps = short_filt.shape[2]
    ctx_count = lax.axis_size("ctx")
    own_index = lax.axis_index("ctx")
    per_device = ctx_count // 2
    piece_rows = rows // per_device
    factor = 1.0 / math.sqrt(rows * ctx_count * GROUP)
    chunk = LANES if width % LANES == 0 else width
    steps = width // chunk
    grid = (steps,)
    near = chunk // GROUP

    def lead3(n):
        return pl.BlockSpec((3, n, chunk), lambda i: (0, 0, i))

    def flat(n):
        return pl.BlockSpec((n, chunk), lambda i: (0, i))

    filt_spec = pl.BlockSpec((near, taps), lambda i: (i, 0))
    f32, half = jnp.float32, features.dtype

    everyone = piece_home.reshape(ctx_count, per_device)
    positions = (piece_start // piece_rows).reshape(ctx_count, per_device)
    local_home = lax.dynamic_slice_in_dim(everyone, own_index, 1, 0)[0]
    device_ids = jnp.arange(ctx_count, dtype=jnp.int32)
    slot_ids = jnp.arange(per_device, dtype=jnp.int32)
    matches = local_home[None, :] == device_ids[:, None]
    send_slot = jnp.sum(jnp.where(matches, slot_ids[None, :], 0), axis=1)
    keyed = jnp.where(everyone == own_index, positions, -1)
    hits = jnp.any(keyed[:, :, None] == slot_ids[None, None, :], axis=1)
    source_of = jnp.sum(jnp.where(hits, device_ids[:, None], 0), axis=0)
    summed = lax.psum_scatter(attn_parts[0], "tp", scatter_dimension=1, tiled=True)
    pieces = summed.reshape(per_device, piece_rows, -1)
    attn_home = lax.all_to_all(
        pieces[send_slot], "ctx", split_axis=0, concat_axis=0, tiled=True
    )[source_of].reshape(rows, -1)

    short_weights = jnp.transpose(jnp.repeat(short_filt, GROUP, axis=1), (0, 2, 1)).astype(f32)
    filt = med_filt.astype(f32)
    filt_back = jnp.roll(filt[:, ::-1], 1, axis=1)
    stream_rim = shifted(features[:, rows - short_taps + 1 :, :], "ctx", 1)
    streams, keyval = call(
        streams_kernel,
        grid,
        [lead3(rows), lead3(short_taps - 1), lead3(short_taps)],
        (lead3(rows), flat(rows)),
        (
            jax.ShapeDtypeStruct((3, rows, width), f32),
            jax.ShapeDtypeStruct((rows, width), half),
        ),
        3 * 14 * rows * width,
        20 * rows * width,
        [pltpu.VMEM((rows + 8, chunk), f32)],
    )(features, stream_rim, short_weights)
    key_rim = shifted(keyval, "ctx", 1)
    mixed = call(
        mixed_kernel,
        grid,
        [filt_spec, flat(rows), flat(rows)],
        flat(rows),
        jax.ShapeDtypeStruct((rows, width), f32),
        4 * groups * taps * taps * chunk,
        8 * rows * width,
    )(filt_back, key_rim, keyval)

    grad = out_grad.astype(f32) + attn_home.astype(f32)
    dmix = (grad * streams[0]).astype(half)
    dquery = grad * mixed
    grad_rim = shifted(dmix, "ctx", -1)
    pair = streams[1:]
    dstreams, med_part, short_cols, heads = call(
        back_kernel,
        grid,
        [
            filt_spec, flat(rows), flat(rows), flat(rows), flat(rows),
            pl.BlockSpec((2, rows, chunk), lambda i: (0, 0, i)),
            flat(rows), lead3(rows), lead3(short_taps - 1),
        ],
        (lead3(rows), filt_spec, lead3(short_taps), lead3(8)),
        (
            jax.ShapeDtypeStruct((3, rows, width), f32),
            jax.ShapeDtypeStruct((groups, taps), f32),
            jax.ShapeDtypeStruct((3, short_taps, width), f32),
            jax.ShapeDtypeStruct((3, 8, width), half),
        ),
        8 * groups * taps * taps * chunk,
        40 * rows * width,
        [pltpu.VMEM((rows + 8, chunk), f32)],
    )(filt, dmix, grad_rim, keyval, key_rim, pair, dquery, features, stream_rim)
    member = (
        jnp.arange(width, dtype=jnp.int32)[:, None] // GROUP
        == jnp.arange(max(groups, taps), dtype=jnp.int32)[None, :]
    ).astype(f32)[:, :taps]
    short_part = jnp.dot(
        short_cols.reshape(3 * short_taps, width), member, precision=lax.Precision.HIGHEST
    )
    used = groups + 3 * short_taps
    share = -(-used // ctx_count)
    parts = jnp.concatenate(
        [med_part, short_part, jnp.zeros((share * ctx_count - used, taps), f32)], axis=0
    ).reshape(ctx_count, share, taps)
    vmem = pl.BlockSpec(memory_space=pltpu.VMEM)
    dma = pltpu.SemaphoreType.DMA
    feat_grad, totals = pl.pallas_call(
        functools.partial(final_kernel, ctx_count),
        in_specs=[vmem] * 4,
        out_specs=(vmem, vmem),
        out_shape=(
            jax.ShapeDtypeStruct((3, rows, width), half),
            jax.ShapeDtypeStruct(parts.shape, f32),
        ),
        scratch_shapes=[
            pltpu.VMEM(parts.shape, f32),
            pltpu.VMEM(parts.shape, f32),
            pltpu.VMEM((3, 8, width), half),
            pltpu.VMEM((rows + 8, chunk), f32),
            dma((ctx_count,)), dma((ctx_count,)), dma((ctx_count,)), dma((ctx_count,)),
            dma, dma,
        ],
        compiler_params=pltpu.CompilerParams(
            collective_id=1, has_side_effects=True, vmem_limit_bytes=32 * 1024 * 1024
        ),
        cost_estimate=cost(3 * 14 * rows * width, 20 * rows * width),
    )(parts, dstreams, heads, short_weights)
    flat_totals = totals.reshape(-1, taps)
    short_total = flat_totals[groups:used, :groups].reshape(3, short_taps, groups)
    return (
        feat_grad,
        jnp.transpose(short_total, (0, 2, 1)) * factor,
        flat_totals[:groups, ::-1] * factor,
    )


def solution(mesh):
    return jax.shard_map(
        shards,
        mesh=mesh,
        in_specs=(
            P(None, "ctx", "tp"),
            P("ctx", "tp"),
            P("tp", "ctx", None),
            P(None, "tp", None),
            P("tp", None),
            P(),
            P(),
        ),
        out_specs=(P(None, "ctx", "tp"), P(None, "tp", None), P("tp", None)),
        check_vma=False,
    )
```

```python
import functools
import math

import jax
import jax.numpy as jnp
from jax import lax
from jax.experimental import pallas as pl
from jax.experimental.pallas import tpu as pltpu
from jax.sharding import PartitionSpec as P

GROUP = 16
MESH = pl.DeviceIdType.MESH
LANES = 256
PARAMS = pltpu.CompilerParams(vmem_limit_bytes=32 * 1024 * 1024)


def shifted(x, axis, by):
    size = lax.axis_size(axis)
    pairs = [(i, i + by) for i in range(size) if 0 <= i + by < size]
    return lax.ppermute(x, axis, pairs)


def cost(flops, bytes_accessed):
    return pl.CostEstimate(flops=flops, bytes_accessed=bytes_accessed, transcendentals=0)


def call(body, grid, in_specs, out_specs, out_shape, flops, moved, scratch=()):
    return pl.pallas_call(
        body,
        grid=grid,
        in_specs=in_specs,
        out_specs=out_specs,
        out_shape=out_shape,
        scratch_shapes=list(scratch),
        compiler_params=PARAMS,
        cost_estimate=cost(flops, moved),
    )


def plane(rows, axis):
    return lax.broadcasted_iota(jnp.int32, (rows, rows), axis)


def front_kernel(
    n, tp, pick_ref, origin_ref, attn_ref, feat_ref, out_grad_ref, wt_ref, filt_ref,
    streams_ref, kv_ref, before_ref, rim_ref, dmix_ref, dq_ref, after_ref,
    got, passed, crossed, acc, pieces, stage, landed, rim_in, key_in, mix_in, ext,
    pair_send, pair_recv, cross_send, cross_recv, send, recv, halo_send, halo_recv,
):
    me = lax.axis_index("ctx")
    col = lax.axis_index("tp")
    f32 = jnp.float32
    rows, width = kv_ref.shape
    taps = wt_ref.shape[1]
    long_taps = filt_ref.shape[1]
    chunk = ext.shape[1]
    piece_rows = stage.shape[1]
    half = tp // 2
    blocks = got.shape[1]
    part = rows // blocks
    side, row = lax.rem(col, 2), col // 2
    partner = row * 2 + 1 - side
    barrier = pltpu.get_barrier_semaphore()

    def other(d):
        return lax.rem(row + d, half) * 2 + side

    def greet(k, carry):
        pl.semaphore_signal(
            barrier, inc=1, device_id={"ctx": lax.rem(me + k, n)}, device_id_type=MESH
        )
        return carry

    lax.fori_loop(1, n, greet, 0)
    pl.semaphore_signal(barrier, inc=1, device_id={"tp": partner}, device_id_type=MESH)
    for d in range(1, half):
        pl.semaphore_signal(barrier, inc=1, device_id={"tp": other(d)}, device_id_type=MESH)
    pl.semaphore_wait(barrier, n - 1 + half)

    def hop(source, target, at, by):
        return pltpu.make_async_remote_copy(
            source, target, halo_send.at[at], halo_recv.at[at],
            device_id={"ctx": lax.rem(me + by + n, n)}, device_id_type=MESH,
        )

    def slab(which, r):
        lane = pl.multiple_of(which * width, width)
        return attn_ref.at[pl.ds(r * part, part), pl.ds(lane, width)]

    def slab_value(which, r):
        lane = pl.multiple_of(which * width, width)
        return attn_ref[pl.ds(r * part, part), pl.ds(lane, width)].astype(f32)

    def pair(d, r):
        line = lax.rem(row + d, half)
        return pltpu.make_async_remote_copy(
            slab(line * 2 + 1 - side, r), got.at[d, r],
            pair_send.at[d, r], pair_recv.at[d, r],
            device_id={"tp": partner}, device_id_type=MESH,
        )

    def cross(d, r):
        return pltpu.make_async_remote_copy(
            passed.at[d, r], crossed.at[d, r], cross_send.at[d, r], cross_recv.at[d, r],
            device_id={"tp": other(d)}, device_id_type=MESH,
        )

    order = [d for d in range(1, half)] + [0]
    rim_hop = hop(feat_ref.at[:, pl.ds(rows - 16, 16), :], rim_in, 0, 1)
    rim_hop.start()
    for d in order:
        for r in range(blocks):
            pair(d, r).start()
    for d in range(1, half):
        for r in range(blocks):
            pair(d, r).wait()
            passed[d, r] = (slab_value(other(d), r) + got[d, r].astype(f32)).astype(got.dtype)
            cross(d, r).start()
    rim_hop.wait()
    first = me == 0
    last = me == n - 1
    rim_ref[...] = jnp.where(first, 0.0, rim_in[...].astype(f32)).astype(rim_ref.dtype)

    def stream_step(c, carry):
        cols = pl.ds(pl.multiple_of(c * chunk, chunk), chunk)
        found = []
        for s in range(3):
            ext[0:16] = rim_ref[s, :, cols].astype(f32)
            ext[16:] = feat_ref[s, :, cols].astype(f32)
            total = wt_ref[s, 0:1, cols] * ext[16:]
            for lag in range(1, taps):
                total = total + wt_ref[s, lag : lag + 1, cols] * ext[16 - lag : 16 - lag + rows]
            streams_ref[s, :, cols] = total
            found.append(total)
        kv_ref[:, cols] = (found[1] * found[2]).astype(kv_ref.dtype)
        return carry

    lax.fori_loop(0, width // chunk, stream_step, 0)
    key_hop = hop(kv_ref, key_in, 1, 1)
    key_hop.start()
    for r in range(blocks):
        pair(0, r).wait()
        total = slab_value(col, r) + got[0, r].astype(f32)
        for d in range(1, half):
            cross(d, r).wait()
            total = total + crossed[d, r].astype(f32)
        for i in range(part // piece_rows):
            pieces[r * (part // piece_rows) + i] = total[i * piece_rows : (i + 1) * piece_rows]

    def route(k):
        peer = lax.rem(me + k, n)
        return pltpu.make_async_remote_copy(
            stage.at[k], landed.at[k], send.at[k], recv.at[k],
            device_id={"ctx": peer}, device_id_type=MESH,
        )

    def piece(k):
        slot = pick_ref[lax.rem(me + k, n)]
        return pieces[slot].astype(stage.dtype)

    def send_step(k, carry):
        stage[k] = piece(k)
        route(k).start()
        return carry

    lax.fori_loop(1, n, send_step, 0)
    landed[0] = piece(0)
    key_hop.wait()
    before_ref[...] = jnp.where(first, 0.0, key_in[...].astype(f32)).astype(before_ref.dtype)
    t, s = plane(long_taps, 0), plane(long_taps, 1)
    owner = lax.broadcasted_iota(jnp.int32, (long_taps, chunk), 1) // GROUP

    def mixed_step(c, carry):
        cols = pl.ds(pl.multiple_of(c * chunk, chunk), chunk)
        window = jnp.concatenate([before_ref[:, cols], kv_ref[:, cols]], axis=0)
        total = jnp.zeros((long_taps, chunk), f32)
        for g in range(chunk // GROUP):
            line = jnp.broadcast_to(
                filt_ref[pl.ds(c * (chunk // GROUP) + g, 1), :], (long_taps, long_taps)
            )
            wheel = pltpu.roll(line, 0, 1, stride=1, stride_axis=0)
            table = jnp.concatenate(
                [jnp.where(s > t, wheel, 0.0), jnp.where(s <= t, wheel, 0.0)], axis=1
            ).astype(kv_ref.dtype)
            product = jnp.dot(table, window, preferred_element_type=f32)
            total = jnp.where(owner == g, product, total)
        dq_ref[:, cols] = total
        return carry

    lax.fori_loop(0, width // chunk, mixed_step, 0)

    def wait_step(k, carry):
        route(k).wait()
        return carry

    lax.fori_loop(1, n, wait_step, 0)

    for slot in range(rows // piece_rows):
        at = lax.rem(me - origin_ref[slot] + n, n)
        acc[slot * piece_rows : (slot + 1) * piece_rows] = landed[at].astype(f32)
    grad = out_grad_ref[...].astype(f32) + acc[...]
    dmix_ref[...] = (grad * streams_ref[0]).astype(dmix_ref.dtype)
    mix_hop = hop(dmix_ref, mix_in, 2, -1)
    mix_hop.start()
    dq_ref[...] = grad * dq_ref[...]
    mix_hop.wait()
    after_ref[...] = jnp.where(last, 0.0, mix_in[...].astype(f32)).astype(after_ref.dtype)


def back_kernel(
    filt_ref, dmix_ref, after_ref, kv_ref, before_ref, streams_ref, dq_ref, feat_ref, rim_ref,
    dstreams_ref, med_ref, short_ref, head_ref, ext,
):
    taps = filt_ref.shape[1]
    width = dmix_ref.shape[1]
    kind = dmix_ref.dtype
    t, s = plane(taps, 0), plane(taps, 1)
    owner = lax.broadcasted_iota(jnp.int32, (taps, width), 1) // GROUP
    dmix = dmix_ref[...]
    window = jnp.concatenate([dmix, after_ref[...]], axis=0)
    flip = jnp.where(t + s == taps - 1, 1.0, 0.0).astype(kind)
    flipped = jnp.dot(flip, dmix, preferred_element_type=jnp.float32)
    keyval = jnp.concatenate([before_ref[...], kv_ref[...]], axis=0)
    total = jnp.zeros((taps, width), jnp.float32)
    for g in range(width // GROUP):
        line = jnp.broadcast_to(filt_ref[g : g + 1, :], (taps, taps))
        wheel = pltpu.roll(line, 0, 1, stride=1, stride_axis=0)
        table = jnp.concatenate(
            [jnp.where(s >= t, wheel, 0.0), jnp.where(s < t, wheel, 0.0)], axis=1
        ).astype(kind)
        product = jnp.dot(table, window, preferred_element_type=jnp.float32)
        total = jnp.where(owner == g, product, total)
        left = jnp.where(owner == g, flipped, 0.0).astype(kind)
        cross = lax.dot_general(
            left, keyval, (((1,), (1,)), ((), ())), preferred_element_type=jnp.float32
        )
        ring = jnp.where(s + t <= taps - 1, cross[:, taps:], cross[:, :taps])
        ring = pltpu.roll(ring, 0, 1, stride=1, stride_axis=0)
        med_ref[g : g + 1, :] = jnp.sum(ring, axis=0, keepdims=True)
    rows = feat_ref.shape[1]
    short_taps = short_ref.shape[1]
    parts = (dq_ref[...], total * streams_ref[1], total * streams_ref[0])
    for k in range(3):
        dstreams_ref[k] = parts[k]
        head_ref[k] = parts[k][:8].astype(head_ref.dtype)
        ext[0:16] = rim_ref[k].astype(jnp.float32)
        ext[16:] = feat_ref[k].astype(jnp.float32)
        for lag in range(short_taps):
            short_ref[k, lag : lag + 1, :] = jnp.sum(
                parts[k] * ext[16 - lag : 16 - lag + rows], axis=0, keepdims=True
            )


def final_kernel(
    n, part_ref, ds_ref, head_ref, wt_ref, feat_ref, total_ref,
    landed, gathered, rim, ext, send1, recv1, send2, recv2, send_rim, recv_rim,
):
    me = lax.axis_index("ctx")
    rows, width = ds_ref.shape[1:]
    taps = wt_ref.shape[1]
    chunk = ext.shape[1]
    barrier = pltpu.get_barrier_semaphore()

    def greet(k, carry):
        pl.semaphore_signal(
            barrier, inc=1, device_id={"ctx": lax.rem(me + k, n)}, device_id_type=MESH
        )
        return carry

    lax.fori_loop(1, n, greet, 0)
    pl.semaphore_wait(barrier, n - 1)

    def scatter(k):
        peer = lax.rem(me + k, n)
        return pltpu.make_async_remote_copy(
            part_ref.at[peer], landed.at[k], send1.at[k], recv1.at[k],
            device_id={"ctx": peer}, device_id_type=MESH,
        )

    def gather(k):
        peer = lax.rem(me + k, n)
        return pltpu.make_async_remote_copy(
            gathered.at[me], gathered.at[me], send2.at[k], recv2.at[k],
            device_id={"ctx": peer}, device_id_type=MESH,
        )

    def each(copy, act):
        def step(k, carry):
            act(copy(k))
            return carry

        lax.fori_loop(1, n, step, 0)

    halo = pltpu.make_async_remote_copy(
        head_ref, rim, send_rim, recv_rim,
        device_id={"ctx": lax.rem(me + n - 1, n)}, device_id_type=MESH,
    )
    halo.start()
    each(scatter, lambda c: c.start())
    landed[0] = part_ref[me]
    each(scatter, lambda c: c.wait())
    total = landed[0]
    for k in range(1, n):
        total = total + landed[k]
    gathered[me] = total
    each(gather, lambda c: c.start())
    halo.wait()
    live = jnp.where(me == n - 1, 0.0, 1.0)
    for s in range(3):
        for c in range(width // chunk):
            cols = slice(c * chunk, (c + 1) * chunk)
            ext[0:rows] = ds_ref[s, :, cols]
            ext[rows : rows + 8] = live * rim[s, :, cols].astype(jnp.float32)
            total = wt_ref[s, 0:1, cols] * ds_ref[s, :, cols]
            for lag in range(1, taps):
                total = total + wt_ref[s, lag : lag + 1, cols] * ext[lag : lag + rows]
            feat_ref[s, :, cols] = total.astype(feat_ref.dtype)
    each(gather, lambda c: c.wait())
    total_ref[...] = gathered[...]


def shards(features, out_grad, attn_parts, short_filt, med_filt, piece_home, piece_start):
    rows, width = out_grad.shape
    groups, taps = med_filt.shape
    short_taps = short_filt.shape[2]
    ctx_count = lax.axis_size("ctx")
    own_index = lax.axis_index("ctx")
    per_device = ctx_count // 2
    piece_rows = rows // per_device
    factor = 1.0 / math.sqrt(rows * ctx_count * GROUP)
    chunk = LANES if width % LANES == 0 else width
    steps = width // chunk
    grid = (steps,)
    near = chunk // GROUP

    def lead3(n):
        return pl.BlockSpec((3, n, chunk), lambda i: (0, 0, i))

    def flat(n):
        return pl.BlockSpec((n, chunk), lambda i: (0, i))

    filt_spec = pl.BlockSpec((near, taps), lambda i: (i, 0))
    f32, half = jnp.float32, features.dtype

    everyone = piece_home.reshape(ctx_count, per_device)
    positions = (piece_start // piece_rows).reshape(ctx_count, per_device)
    local_home = lax.dynamic_slice_in_dim(everyone, own_index, 1, 0)[0]
    device_ids = jnp.arange(ctx_count, dtype=jnp.int32)
    slot_ids = jnp.arange(per_device, dtype=jnp.int32)
    matches = local_home[None, :] == device_ids[:, None]
    send_slot = jnp.sum(jnp.where(matches, slot_ids[None, :], 0), axis=1)
    keyed = jnp.where(everyone == own_index, positions, -1)
    hits = jnp.any(keyed[:, :, None] == slot_ids[None, None, :], axis=1)
    source_of = jnp.sum(jnp.where(hits, device_ids[:, None], 0), axis=0)
    short_weights = jnp.transpose(jnp.repeat(short_filt, GROUP, axis=1), (0, 2, 1)).astype(f32)
    filt = med_filt.astype(f32)
    filt_back = jnp.roll(filt[:, ::-1], 1, axis=1)
    tp_count = lax.axis_size("tp")
    blocks = 2 if rows % 32 == 0 else 1
    vmem = pl.BlockSpec(memory_space=pltpu.VMEM)
    smem = pl.BlockSpec(memory_space=pltpu.SMEM)
    dma = pltpu.SemaphoreType.DMA
    lanes = jax.ShapeDtypeStruct((rows, width), half)
    crossing = pltpu.VMEM((tp_count // 2, blocks, rows // blocks, width), half)
    flags = dma((tp_count // 2, blocks))
    routed = pltpu.VMEM((ctx_count, piece_rows, width), half)
    streams, keyval, key_rim, stream_rim, dmix, dquery, grad_rim = pl.pallas_call(
        functools.partial(front_kernel, ctx_count, tp_count),
        in_specs=[smem, smem] + [vmem] * 5,
        out_specs=(vmem,) * 7,
        out_shape=(
            jax.ShapeDtypeStruct((3, rows, width), f32),
            lanes,
            lanes,
            jax.ShapeDtypeStruct((3, 16, width), half),
            lanes,
            jax.ShapeDtypeStruct((rows, width), f32),
            lanes,
        ),
        scratch_shapes=[
            crossing, crossing, crossing,
            pltpu.VMEM((rows, width), f32),
            pltpu.VMEM((per_device, piece_rows, width), f32),
            routed, routed,
            pltpu.VMEM((3, 16, width), half),
            pltpu.VMEM((rows, width), half),
            pltpu.VMEM((rows, width), half),
            pltpu.VMEM((rows + 16, chunk), f32),
            flags, flags, flags, flags,
            dma((ctx_count,)), dma((ctx_count,)), dma((3,)), dma((3,)),
        ],
        compiler_params=pltpu.CompilerParams(
            collective_id=0, has_side_effects=True, vmem_limit_bytes=48 * 1024 * 1024
        ),
        cost_estimate=cost(4 * groups * taps * taps * chunk, 40 * rows * width),
    )(
        send_slot.astype(jnp.int32), source_of.astype(jnp.int32), attn_parts[0], features,
        out_grad, short_weights, filt_back,
    )
    pair = streams[1:]
    dstreams, med_part, short_cols, heads = call(
        back_kernel,
        grid,
        [
            filt_spec, flat(rows), flat(rows), flat(rows), flat(rows),
            pl.BlockSpec((2, rows, chunk), lambda i: (0, 0, i)),
            flat(rows), lead3(rows), lead3(16),
        ],
        (lead3(rows), filt_spec, lead3(short_taps), lead3(8)),
        (
            jax.ShapeDtypeStruct((3, rows, width), f32),
            jax.ShapeDtypeStruct((groups, taps), f32),
            jax.ShapeDtypeStruct((3, short_taps, width), f32),
            jax.ShapeDtypeStruct((3, 8, width), half),
        ),
        8 * groups * taps * taps * chunk,
        40 * rows * width,
        [pltpu.VMEM((rows + 16, chunk), f32)],
    )(filt, dmix, grad_rim, keyval, key_rim, pair, dquery, features, stream_rim)
    member = (
        jnp.arange(width, dtype=jnp.int32)[:, None] // GROUP
        == jnp.arange(max(groups, taps), dtype=jnp.int32)[None, :]
    ).astype(f32)[:, :taps]
    short_part = jnp.dot(
        short_cols.reshape(3 * short_taps, width), member, precision=lax.Precision.HIGHEST
    )
    used = groups + 3 * short_taps
    share = -(-used // ctx_count)
    parts = jnp.concatenate(
        [med_part, short_part, jnp.zeros((share * ctx_count - used, taps), f32)], axis=0
    ).reshape(ctx_count, share, taps)
    vmem = pl.BlockSpec(memory_space=pltpu.VMEM)
    dma = pltpu.SemaphoreType.DMA
    feat_grad, totals = pl.pallas_call(
        functools.partial(final_kernel, ctx_count),
        in_specs=[vmem] * 4,
        out_specs=(vmem, vmem),
        out_shape=(
            jax.ShapeDtypeStruct((3, rows, width), half),
            jax.ShapeDtypeStruct(parts.shape, f32),
        ),
        scratch_shapes=[
            pltpu.VMEM(parts.shape, f32),
            pltpu.VMEM(parts.shape, f32),
            pltpu.VMEM((3, 8, width), half),
            pltpu.VMEM((rows + 8, chunk), f32),
            dma((ctx_count,)), dma((ctx_count,)), dma((ctx_count,)), dma((ctx_count,)),
            dma, dma,
        ],
        compiler_params=pltpu.CompilerParams(
            collective_id=1, has_side_effects=True, vmem_limit_bytes=32 * 1024 * 1024
        ),
        cost_estimate=cost(3 * 14 * rows * width, 20 * rows * width),
    )(parts, dstreams, heads, short_weights)
    flat_totals = totals.reshape(-1, taps)
    short_total = flat_totals[groups:used, :groups].reshape(3, short_taps, groups)
    return (
        feat_grad,
        jnp.transpose(short_total, (0, 2, 1)) * factor,
        flat_totals[:groups, ::-1] * factor,
    )


def solution(mesh):
    return jax.shard_map(
        shards,
        mesh=mesh,
        in_specs=(
            P(None, "ctx", "tp"),
            P("ctx", "tp"),
            P("tp", "ctx", None),
            P(None, "tp", None),
            P("tp", None),
            P(),
            P(),
        ),
        out_specs=(P(None, "ctx", "tp"), P(None, "tp", None), P("tp", None)),
        check_vma=False,
    )
```

```python
import functools
import math

import jax
import jax.numpy as jnp
from jax import lax
from jax.experimental import pallas as pl
from jax.experimental.pallas import tpu as pltpu
from jax.sharding import PartitionSpec as P

GROUP = 16
MESH = pl.DeviceIdType.MESH
LANES = 256


def cost(flops, bytes_accessed):
    return pl.CostEstimate(flops=flops, bytes_accessed=bytes_accessed, transcendentals=0)


def plane(rows, axis):
    return lax.broadcasted_iota(jnp.int32, (rows, rows), axis)


def whole_kernel(
    n, tp, pick_ref, origin_ref, attn_ref, feat_ref, out_grad_ref, wt_ref, filt_ref, back_ref,
    feat_out, total_ref,
    streams_ref, kv_ref, before_ref, rim_ref, dmix_ref, ds_ref, after_ref,
    short_ref, flat_ref, part_ref, sums, gathered, head_ref, tail_in,
    got, passed, crossed, acc, pieces, stage, landed, rim_in, key_in, mix_in, ext,
    pair_send, pair_recv, cross_send, cross_recv, send, recv, halo_send, halo_recv,
    send1, recv1, send2, recv2,
):
    dq_ref = ds_ref.at[0]
    me = lax.axis_index("ctx")
    col = lax.axis_index("tp")
    f32 = jnp.float32
    rows, width = kv_ref.shape
    taps = wt_ref.shape[1]
    long_taps = filt_ref.shape[1]
    chunk = ext.shape[1]
    piece_rows = stage.shape[1]
    half = tp // 2
    blocks = got.shape[1]
    part = rows // blocks
    side, row = lax.rem(col, 2), col // 2
    partner = row * 2 + 1 - side
    barrier = pltpu.get_barrier_semaphore()

    def other(d):
        return lax.rem(row + d, half) * 2 + side

    def greet(k, carry):
        pl.semaphore_signal(
            barrier, inc=1, device_id={"ctx": lax.rem(me + k, n)}, device_id_type=MESH
        )
        return carry

    lax.fori_loop(1, n, greet, 0)
    pl.semaphore_signal(barrier, inc=1, device_id={"tp": partner}, device_id_type=MESH)
    for d in range(1, half):
        pl.semaphore_signal(barrier, inc=1, device_id={"tp": other(d)}, device_id_type=MESH)
    pl.semaphore_wait(barrier, n - 1 + half)

    def hop(source, target, at, by):
        return pltpu.make_async_remote_copy(
            source, target, halo_send.at[at], halo_recv.at[at],
            device_id={"ctx": lax.rem(me + by + n, n)}, device_id_type=MESH,
        )

    def slab(which, r):
        lane = pl.multiple_of(which * width, width)
        return attn_ref.at[pl.ds(r * part, part), pl.ds(lane, width)]

    def slab_value(which, r):
        lane = pl.multiple_of(which * width, width)
        return attn_ref[pl.ds(r * part, part), pl.ds(lane, width)].astype(f32)

    def pair(d, r):
        line = lax.rem(row + d, half)
        return pltpu.make_async_remote_copy(
            slab(line * 2 + 1 - side, r), got.at[d, r],
            pair_send.at[d, r], pair_recv.at[d, r],
            device_id={"tp": partner}, device_id_type=MESH,
        )

    def cross(d, r):
        return pltpu.make_async_remote_copy(
            passed.at[d, r], crossed.at[d, r], cross_send.at[d, r], cross_recv.at[d, r],
            device_id={"tp": other(d)}, device_id_type=MESH,
        )

    order = [d for d in range(1, half)] + [0]
    rim_hop = hop(feat_ref.at[:, pl.ds(rows - 16, 16), :], rim_in, 0, 1)
    rim_hop.start()
    for d in order:
        for r in range(blocks):
            pair(d, r).start()
    for d in range(1, half):
        for r in range(blocks):
            pair(d, r).wait()
            passed[d, r] = (slab_value(other(d), r) + got[d, r].astype(f32)).astype(got.dtype)
            cross(d, r).start()
    rim_hop.wait()
    first = me == 0
    last = me == n - 1
    rim_ref[...] = jnp.where(first, 0.0, rim_in[...].astype(f32)).astype(rim_ref.dtype)

    def stream_step(c, carry):
        cols = pl.ds(pl.multiple_of(c * chunk, chunk), chunk)
        found = []
        for s in range(3):
            ext[0:16] = rim_ref[s, :, cols].astype(f32)
            ext[16:] = feat_ref[s, :, cols].astype(f32)
            total = wt_ref[s, 0:1, cols] * ext[16:]
            for lag in range(1, taps):
                total = total + wt_ref[s, lag : lag + 1, cols] * ext[16 - lag : 16 - lag + rows]
            streams_ref[s, :, cols] = total
            found.append(total)
        kv_ref[:, cols] = (found[1] * found[2]).astype(kv_ref.dtype)
        return carry

    lax.fori_loop(0, width // chunk, stream_step, 0)
    key_hop = hop(kv_ref, key_in, 1, 1)
    key_hop.start()
    for r in range(blocks):
        pair(0, r).wait()
        total = slab_value(col, r) + got[0, r].astype(f32)
        for d in range(1, half):
            cross(d, r).wait()
            total = total + crossed[d, r].astype(f32)
        for i in range(part // piece_rows):
            pieces[r * (part // piece_rows) + i] = total[i * piece_rows : (i + 1) * piece_rows]

    def route(k):
        peer = lax.rem(me + k, n)
        return pltpu.make_async_remote_copy(
            stage.at[k], landed.at[k], send.at[k], recv.at[k],
            device_id={"ctx": peer}, device_id_type=MESH,
        )

    def piece(k):
        slot = pick_ref[lax.rem(me + k, n)]
        return pieces[slot].astype(stage.dtype)

    def send_step(k, carry):
        stage[k] = piece(k)
        route(k).start()
        return carry

    lax.fori_loop(1, n, send_step, 0)
    landed[0] = piece(0)
    key_hop.wait()
    before_ref[...] = jnp.where(first, 0.0, key_in[...].astype(f32)).astype(before_ref.dtype)
    t, s = plane(long_taps, 0), plane(long_taps, 1)
    owner = lax.broadcasted_iota(jnp.int32, (long_taps, chunk), 1) // GROUP

    def mixed_step(c, carry):
        cols = pl.ds(pl.multiple_of(c * chunk, chunk), chunk)
        window = jnp.concatenate([before_ref[:, cols], kv_ref[:, cols]], axis=0)
        total = jnp.zeros((long_taps, chunk), f32)
        for g in range(chunk // GROUP):
            line = jnp.broadcast_to(
                filt_ref[pl.ds(c * (chunk // GROUP) + g, 1), :], (long_taps, long_taps)
            )
            wheel = pltpu.roll(line, 0, 1, stride=1, stride_axis=0)
            table = jnp.concatenate(
                [jnp.where(s > t, wheel, 0.0), jnp.where(s <= t, wheel, 0.0)], axis=1
            ).astype(kv_ref.dtype)
            product = jnp.dot(table, window, preferred_element_type=f32)
            total = jnp.where(owner == g, product, total)
        dq_ref[:, cols] = total
        return carry

    lax.fori_loop(0, width // chunk, mixed_step, 0)

    def wait_step(k, carry):
        route(k).wait()
        return carry

    lax.fori_loop(1, n, wait_step, 0)

    for slot in range(rows // piece_rows):
        at = lax.rem(me - origin_ref[slot] + n, n)
        acc[slot * piece_rows : (slot + 1) * piece_rows] = landed[at].astype(f32)
    grad = out_grad_ref[...].astype(f32) + acc[...]
    dmix_ref[...] = (grad * streams_ref[0]).astype(dmix_ref.dtype)
    mix_hop = hop(dmix_ref, mix_in, 2, -1)
    mix_hop.start()
    dq_ref[...] = grad * dq_ref[...]
    kind = dmix_ref.dtype
    flip = jnp.where(t + s == long_taps - 1, 1.0, 0.0).astype(kind)
    near = chunk // GROUP

    def short_sums(k, cols, value):
        ext[0:16] = rim_ref[k, :, cols].astype(f32)
        ext[16:] = feat_ref[k, :, cols].astype(f32)
        for lag in range(taps):
            at = k * taps + lag
            short_ref[at : at + 1, cols] = jnp.sum(
                value * ext[16 - lag : 16 - lag + rows], axis=0, keepdims=True
            )

    def lag_step(c, carry):
        cols = pl.ds(pl.multiple_of(c * chunk, chunk), chunk)
        flipped = jnp.dot(flip, dmix_ref[:, cols], preferred_element_type=f32)
        window = jnp.concatenate([before_ref[:, cols], kv_ref[:, cols]], axis=0)
        for g in range(near):
            left = jnp.where(owner == g, flipped, 0.0).astype(kind)
            both = lax.dot_general(
                left, window, (((1,), (1,)), ((), ())), preferred_element_type=f32
            )
            ring = jnp.where(s + t <= long_taps - 1, both[:, long_taps:], both[:, :long_taps])
            ring = pltpu.roll(ring, 0, 1, stride=1, stride_axis=0)
            flat_ref[pl.ds(c * near + g, 1), :] = jnp.sum(ring, axis=0, keepdims=True)
        short_sums(0, cols, dq_ref[:, cols])
        return carry

    lax.fori_loop(0, width // chunk, lag_step, 0)
    mix_hop.wait()
    after_ref[...] = jnp.where(last, 0.0, mix_in[...].astype(f32)).astype(kind)

    def back_step(c, carry):
        cols = pl.ds(pl.multiple_of(c * chunk, chunk), chunk)
        window = jnp.concatenate([dmix_ref[:, cols], after_ref[:, cols]], axis=0)
        total = jnp.zeros((long_taps, chunk), f32)
        for g in range(near):
            line = jnp.broadcast_to(
                back_ref[pl.ds(c * near + g, 1), :], (long_taps, long_taps)
            )
            wheel = pltpu.roll(line, 0, 1, stride=1, stride_axis=0)
            table = jnp.concatenate(
                [jnp.where(s >= t, wheel, 0.0), jnp.where(s < t, wheel, 0.0)], axis=1
            ).astype(kind)
            product = jnp.dot(table, window, preferred_element_type=f32)
            total = jnp.where(owner == g, product, total)
        for k in (1, 2):
            value = total * streams_ref[3 - k, :, cols]
            ds_ref[k, :, cols] = value
            short_sums(k, cols, value)
        return carry

    lax.fori_loop(0, width // chunk, back_step, 0)
    head_ref[...] = ds_ref[:, 0:16, :].astype(kind)
    tail_hop = hop(head_ref, tail_in, 3, -1)
    tail_hop.start()
    groups = width // GROUP
    used = groups + 3 * taps
    member = jnp.where(
        lax.broadcasted_iota(jnp.int32, (width, long_taps), 0) // GROUP
        == lax.broadcasted_iota(jnp.int32, (width, long_taps), 1),
        1.0,
        0.0,
    )
    flat_ref[groups:used] = jnp.dot(
        short_ref[...], member, precision=lax.Precision.HIGHEST, preferred_element_type=f32
    )
    share = part_ref.shape[1]
    if n * share > used:
        flat_ref[used : n * share] = jnp.zeros((n * share - used, long_taps), f32)
    for k in range(n):
        part_ref[k] = flat_ref[k * share : (k + 1) * share]

    def scatter(k):
        peer = lax.rem(me + k, n)
        return pltpu.make_async_remote_copy(
            part_ref.at[peer], sums.at[k], send1.at[k], recv1.at[k],
            device_id={"ctx": peer}, device_id_type=MESH,
        )

    def gather(k):
        return pltpu.make_async_remote_copy(
            gathered.at[me], gathered.at[me], send2.at[k], recv2.at[k],
            device_id={"ctx": lax.rem(me + k, n)}, device_id_type=MESH,
        )

    def each(copy, act):
        def step(k, carry):
            act(copy(k))
            return carry

        lax.fori_loop(1, n, step, 0)

    def feat_step(k):
        def step(c, carry):
            cols = pl.ds(pl.multiple_of(c * chunk, chunk), chunk)
            ext[0:rows] = ds_ref[k, :, cols]
            ext[rows:] = jnp.where(last, 0.0, tail_in[k, :, cols].astype(f32))
            total = wt_ref[k, 0:1, cols] * ds_ref[k, :, cols]
            for lag in range(1, taps):
                total = total + wt_ref[k, lag : lag + 1, cols] * ext[lag : lag + rows]
            feat_out[k, :, cols] = total.astype(feat_out.dtype)
            return carry

        lax.fori_loop(0, width // chunk, step, 0)

    each(scatter, lambda c: c.start())
    sums[0] = part_ref[me]
    tail_hop.wait()
    feat_step(0)
    each(scatter, lambda c: c.wait())
    result = sums[0]
    for k in range(1, n):
        result = result + sums[k]
    gathered[me] = result
    each(gather, lambda c: c.start())
    feat_step(1)
    feat_step(2)
    each(gather, lambda c: c.wait())
    total_ref[...] = gathered[...]


def shards(features, out_grad, attn_parts, short_filt, med_filt, piece_home, piece_start):
    rows, width = out_grad.shape
    groups, taps = med_filt.shape
    short_taps = short_filt.shape[2]
    ctx_count = lax.axis_size("ctx")
    own_index = lax.axis_index("ctx")
    per_device = ctx_count // 2
    piece_rows = rows // per_device
    factor = 1.0 / math.sqrt(rows * ctx_count * GROUP)
    chunk = LANES if width % LANES == 0 else width
    f32, half = jnp.float32, features.dtype

    everyone = piece_home.reshape(ctx_count, per_device)
    positions = (piece_start // piece_rows).reshape(ctx_count, per_device)
    local_home = lax.dynamic_slice_in_dim(everyone, own_index, 1, 0)[0]
    device_ids = jnp.arange(ctx_count, dtype=jnp.int32)
    slot_ids = jnp.arange(per_device, dtype=jnp.int32)
    matches = local_home[None, :] == device_ids[:, None]
    send_slot = jnp.sum(jnp.where(matches, slot_ids[None, :], 0), axis=1)
    keyed = jnp.where(everyone == own_index, positions, -1)
    hits = jnp.any(keyed[:, :, None] == slot_ids[None, None, :], axis=1)
    source_of = jnp.sum(jnp.where(hits, device_ids[:, None], 0), axis=0)
    short_weights = jnp.transpose(jnp.repeat(short_filt, GROUP, axis=1), (0, 2, 1)).astype(f32)
    filt = med_filt.astype(f32)
    filt_back = jnp.roll(filt[:, ::-1], 1, axis=1)
    tp_count = lax.axis_size("tp")
    blocks = 2 if rows % 32 == 0 else 1
    vmem = pl.BlockSpec(memory_space=pltpu.VMEM)
    smem = pl.BlockSpec(memory_space=pltpu.SMEM)
    dma = pltpu.SemaphoreType.DMA
    lanes = jax.ShapeDtypeStruct((rows, width), half)
    crossing = pltpu.VMEM((tp_count // 2, blocks, rows // blocks, width), half)
    flags = dma((tp_count // 2, blocks))
    routed = pltpu.VMEM((ctx_count, piece_rows, width), half)
    used = groups + 3 * short_taps
    share = -(-used // ctx_count)
    parts = (ctx_count, share, taps)
    held = pltpu.VMEM((rows, width), half)
    heads = pltpu.VMEM((3, 16, width), half)
    wide = pltpu.VMEM((3, rows, width), f32)
    peers = dma((ctx_count,))
    feat_grad, totals = pl.pallas_call(
        functools.partial(whole_kernel, ctx_count, tp_count),
        in_specs=[smem, smem] + [vmem] * 6,
        out_specs=(vmem, vmem),
        out_shape=(
            jax.ShapeDtypeStruct((3, rows, width), half),
            jax.ShapeDtypeStruct(parts, f32),
        ),
        scratch_shapes=[
            wide, held, held, heads, held, wide, held,
            pltpu.VMEM((3 * short_taps, width), f32),
            pltpu.VMEM((ctx_count * share, taps), f32),
            pltpu.VMEM(parts, f32), pltpu.VMEM(parts, f32), pltpu.VMEM(parts, f32),
            heads, heads,
            crossing, crossing, crossing,
            pltpu.VMEM((rows, width), f32),
            pltpu.VMEM((per_device, piece_rows, width), f32),
            routed, routed,
            heads, held, held,
            pltpu.VMEM((rows + 16, chunk), f32),
            flags, flags, flags, flags,
            peers, peers, dma((4,)), dma((4,)),
            peers, peers, peers, peers,
        ],
        compiler_params=pltpu.CompilerParams(
            collective_id=0, has_side_effects=True, vmem_limit_bytes=48 * 1024 * 1024
        ),
        cost_estimate=cost(12 * groups * taps * taps * chunk, 40 * rows * width),
    )(
        send_slot.astype(jnp.int32), source_of.astype(jnp.int32), attn_parts[0], features,
        out_grad, short_weights, filt_back, filt,
    )
    flat_totals = totals.reshape(-1, taps)
    short_total = flat_totals[groups:used, :groups].reshape(3, short_taps, groups)
    return (
        feat_grad,
        jnp.transpose(short_total, (0, 2, 1)) * factor,
        flat_totals[:groups, ::-1] * factor,
    )


def solution(mesh):
    return jax.shard_map(
        shards,
        mesh=mesh,
        in_specs=(
            P(None, "ctx", "tp"),
            P("ctx", "tp"),
            P("tp", "ctx", None),
            P(None, "tp", None),
            P("tp", None),
            P(),
            P(),
        ),
        out_specs=(P(None, "ctx", "tp"), P(None, "tp", None), P("tp", None)),
        check_vma=False,
    )
```

```python
import functools
import math

import jax
import jax.numpy as jnp
from jax import lax
from jax.experimental import pallas as pl
from jax.experimental.pallas import tpu as pltpu
from jax.sharding import PartitionSpec as P

GROUP = 16
MESH = pl.DeviceIdType.MESH
LANES = 256


def cost(flops, bytes_accessed):
    return pl.CostEstimate(flops=flops, bytes_accessed=bytes_accessed, transcendentals=0)


def plane(rows, axis):
    return lax.broadcasted_iota(jnp.int32, (rows, rows), axis)


def whole_kernel(
    n, tp, pick_ref, origin_ref, attn_ref, feat_ref, out_grad_ref, taps_ref, filt_ref, back_ref,
    feat_out, total_ref,
    streams_ref, kv_ref, before_ref, rim_ref, dmix_ref, ds_ref, after_ref,
    wt_ref, table_ref, short_ref, flat_ref, part_ref, sums, gathered, head_ref, tail_in,
    got, passed, crossed, acc, pieces, stage, landed, rim_in, key_in, mix_in, ext,
    pair_send, pair_recv, cross_send, cross_recv, send, recv, halo_send, halo_recv,
    send1, recv1, send2, recv2,
):
    dq_ref = ds_ref.at[0]
    me = lax.axis_index("ctx")
    col = lax.axis_index("tp")
    f32 = jnp.float32
    rows, width = kv_ref.shape
    taps = wt_ref.shape[1]
    long_taps = filt_ref.shape[1]
    chunk = ext.shape[1]
    piece_rows = stage.shape[1]
    half = tp // 2
    blocks = got.shape[1]
    part = rows // blocks
    side, row = lax.rem(col, 2), col // 2
    partner = row * 2 + 1 - side
    barrier = pltpu.get_barrier_semaphore()

    def other(d):
        return lax.rem(row + d, half) * 2 + side

    def greet(k, carry):
        pl.semaphore_signal(
            barrier, inc=1, device_id={"ctx": lax.rem(me + k, n)}, device_id_type=MESH
        )
        return carry

    lax.fori_loop(1, n, greet, 0)
    pl.semaphore_signal(barrier, inc=1, device_id={"tp": partner}, device_id_type=MESH)
    for d in range(1, half):
        pl.semaphore_signal(barrier, inc=1, device_id={"tp": other(d)}, device_id_type=MESH)
    pl.semaphore_wait(barrier, n - 1 + half)

    def hop(source, target, at, by):
        return pltpu.make_async_remote_copy(
            source, target, halo_send.at[at], halo_recv.at[at],
            device_id={"ctx": lax.rem(me + by + n, n)}, device_id_type=MESH,
        )

    def slab(which, r):
        lane = pl.multiple_of(which * width, width)
        return attn_ref.at[pl.ds(r * part, part), pl.ds(lane, width)]

    def slab_value(which, r):
        lane = pl.multiple_of(which * width, width)
        return attn_ref[pl.ds(r * part, part), pl.ds(lane, width)].astype(f32)

    def pair(d, r):
        line = lax.rem(row + d, half)
        return pltpu.make_async_remote_copy(
            slab(line * 2 + 1 - side, r), got.at[d, r],
            pair_send.at[d, r], pair_recv.at[d, r],
            device_id={"tp": partner}, device_id_type=MESH,
        )

    def cross(d, r):
        return pltpu.make_async_remote_copy(
            passed.at[d, r], crossed.at[d, r], cross_send.at[d, r], cross_recv.at[d, r],
            device_id={"tp": other(d)}, device_id_type=MESH,
        )

    order = [d for d in range(1, half)] + [0]
    rim_hop = hop(feat_ref.at[:, pl.ds(rows - 16, 16), :], rim_in, 0, 1)
    rim_hop.start()
    for d in order:
        for r in range(blocks):
            pair(d, r).start()
    for d in range(1, half):
        for r in range(blocks):
            pair(d, r).wait()
            passed[d, r] = (slab_value(other(d), r) + got[d, r].astype(f32)).astype(got.dtype)
            cross(d, r).start()
    spread = jnp.where(
        lax.broadcasted_iota(jnp.int32, (width // GROUP, width), 1) // GROUP
        == lax.broadcasted_iota(jnp.int32, (width // GROUP, width), 0),
        1.0,
        0.0,
    ).astype(taps_ref.dtype)
    weights = jnp.dot(taps_ref[...], spread, preferred_element_type=f32)
    for k in range(3):
        wt_ref[k] = weights[k * taps : (k + 1) * taps]
    rim_hop.wait()
    first = me == 0
    last = me == n - 1
    rim_ref[...] = jnp.where(first, 0.0, rim_in[...].astype(f32)).astype(rim_ref.dtype)

    def stream_step(c, carry):
        cols = pl.ds(pl.multiple_of(c * chunk, chunk), chunk)
        found = []
        for s in range(3):
            ext[0:16] = rim_ref[s, :, cols].astype(f32)
            ext[16:] = feat_ref[s, :, cols].astype(f32)
            total = wt_ref[s, 0:1, cols] * ext[16:]
            for lag in range(1, taps):
                total = total + wt_ref[s, lag : lag + 1, cols] * ext[16 - lag : 16 - lag + rows]
            streams_ref[s, :, cols] = total
            found.append(total)
        kv_ref[:, cols] = (found[1] * found[2]).astype(kv_ref.dtype)
        return carry

    lax.fori_loop(0, width // chunk, stream_step, 0)
    key_hop = hop(kv_ref, key_in, 1, 1)
    key_hop.start()
    for r in range(blocks):
        pair(0, r).wait()
        total = slab_value(col, r) + got[0, r].astype(f32)
        for d in range(1, half):
            cross(d, r).wait()
            total = total + crossed[d, r].astype(f32)
        for i in range(part // piece_rows):
            pieces[r * (part // piece_rows) + i] = total[i * piece_rows : (i + 1) * piece_rows]

    def route(k):
        peer = lax.rem(me + k, n)
        return pltpu.make_async_remote_copy(
            stage.at[k], landed.at[k], send.at[k], recv.at[k],
            device_id={"ctx": peer}, device_id_type=MESH,
        )

    def piece(k):
        slot = pick_ref[lax.rem(me + k, n)]
        return pieces[slot].astype(stage.dtype)

    def send_step(k, carry):
        stage[k] = piece(k)
        route(k).start()
        return carry

    lax.fori_loop(1, n, send_step, 0)
    landed[0] = piece(0)
    key_hop.wait()
    before_ref[...] = jnp.where(first, 0.0, key_in[...].astype(f32)).astype(before_ref.dtype)
    t, s = plane(long_taps, 0), plane(long_taps, 1)
    owner = lax.broadcasted_iota(jnp.int32, (long_taps, chunk), 1) // GROUP

    def mixed_step(c, carry):
        cols = pl.ds(pl.multiple_of(c * chunk, chunk), chunk)
        window = jnp.concatenate([before_ref[:, cols], kv_ref[:, cols]], axis=0)
        total = jnp.zeros((long_taps, chunk), f32)
        for g in range(chunk // GROUP):
            line = jnp.broadcast_to(
                filt_ref[pl.ds(c * (chunk // GROUP) + g, 1), :], (long_taps, long_taps)
            )
            wheel = pltpu.roll(line, 0, 1, stride=1, stride_axis=0)
            table = jnp.concatenate(
                [jnp.where(s > t, wheel, 0.0), jnp.where(s <= t, wheel, 0.0)], axis=1
            ).astype(kv_ref.dtype)
            product = jnp.dot(table, window, preferred_element_type=f32)
            total = jnp.where(owner == g, product, total)
        dq_ref[:, cols] = total
        return carry

    lax.fori_loop(0, width // chunk, mixed_step, 0)

    def table_step(g, carry):
        line = jnp.broadcast_to(back_ref[pl.ds(g, 1), :], (long_taps, long_taps))
        wheel = pltpu.roll(line, 0, 1, stride=1, stride_axis=0)
        table_ref[g] = jnp.concatenate(
            [jnp.where(s >= t, wheel, 0.0), jnp.where(s < t, wheel, 0.0)], axis=1
        ).astype(kv_ref.dtype)
        return carry

    lax.fori_loop(0, width // GROUP, table_step, 0)

    def wait_step(k, carry):
        route(k).wait()
        return carry

    lax.fori_loop(1, n, wait_step, 0)

    for slot in range(rows // piece_rows):
        at = lax.rem(me - origin_ref[slot] + n, n)
        acc[slot * piece_rows : (slot + 1) * piece_rows] = landed[at].astype(f32)
    grad = out_grad_ref[...].astype(f32) + acc[...]
    dmix_ref[...] = (grad * streams_ref[0]).astype(dmix_ref.dtype)
    mix_hop = hop(dmix_ref, mix_in, 2, -1)
    mix_hop.start()
    dq_ref[...] = grad * dq_ref[...]
    kind = dmix_ref.dtype
    flip = jnp.where(t + s == long_taps - 1, 1.0, 0.0).astype(kind)
    near = chunk // GROUP

    def short_sums(k, cols, value):
        ext[0:16] = rim_ref[k, :, cols].astype(f32)
        ext[16:] = feat_ref[k, :, cols].astype(f32)
        for lag in range(taps):
            at = k * taps + lag
            short_ref[at : at + 1, cols] = jnp.sum(
                value * ext[16 - lag : 16 - lag + rows], axis=0, keepdims=True
            )

    def lag_step(c, carry):
        cols = pl.ds(pl.multiple_of(c * chunk, chunk), chunk)
        flipped = jnp.dot(flip, dmix_ref[:, cols], preferred_element_type=f32)
        window = jnp.concatenate([before_ref[:, cols], kv_ref[:, cols]], axis=0)
        for g in range(near):
            left = jnp.where(owner == g, flipped, 0.0).astype(kind)
            both = lax.dot_general(
                left, window, (((1,), (1,)), ((), ())), preferred_element_type=f32
            )
            ring = jnp.where(s + t <= long_taps - 1, both[:, long_taps:], both[:, :long_taps])
            ring = pltpu.roll(ring, 0, 1, stride=1, stride_axis=0)
            flat_ref[pl.ds(c * near + g, 1), :] = jnp.sum(ring, axis=0, keepdims=True)
        short_sums(0, cols, dq_ref[:, cols])
        return carry

    lax.fori_loop(0, width // chunk, lag_step, 0)
    mix_hop.wait()
    after_ref[...] = jnp.where(last, 0.0, mix_in[...].astype(f32)).astype(kind)

    def back_step(c, carry):
        cols = pl.ds(pl.multiple_of(c * chunk, chunk), chunk)
        window = jnp.concatenate([dmix_ref[:, cols], after_ref[:, cols]], axis=0)
        total = jnp.zeros((long_taps, chunk), f32)
        for g in range(near):
            table = table_ref[c * near + g]
            product = jnp.dot(table, window, preferred_element_type=f32)
            total = jnp.where(owner == g, product, total)
        for k in (1, 2):
            value = total * streams_ref[3 - k, :, cols]
            ds_ref[k, :, cols] = value
            short_sums(k, cols, value)
        return carry

    lax.fori_loop(0, width // chunk, back_step, 0)
    head_ref[...] = ds_ref[:, 0:16, :].astype(kind)
    tail_hop = hop(head_ref, tail_in, 3, -1)
    tail_hop.start()
    groups = width // GROUP
    used = groups + 3 * taps
    member = jnp.where(
        lax.broadcasted_iota(jnp.int32, (width, long_taps), 0) // GROUP
        == lax.broadcasted_iota(jnp.int32, (width, long_taps), 1),
        1.0,
        0.0,
    )
    flat_ref[groups:used] = jnp.dot(
        short_ref[...], member, precision=lax.Precision.HIGHEST, preferred_element_type=f32
    )
    share = part_ref.shape[1]
    if n * share > used:
        flat_ref[used : n * share] = jnp.zeros((n * share - used, long_taps), f32)
    for k in range(n):
        part_ref[k] = flat_ref[k * share : (k + 1) * share]

    def scatter(k):
        peer = lax.rem(me + k, n)
        return pltpu.make_async_remote_copy(
            part_ref.at[peer], sums.at[k], send1.at[k], recv1.at[k],
            device_id={"ctx": peer}, device_id_type=MESH,
        )

    def gather(k):
        return pltpu.make_async_remote_copy(
            gathered.at[me], gathered.at[me], send2.at[k], recv2.at[k],
            device_id={"ctx": lax.rem(me + k, n)}, device_id_type=MESH,
        )

    def each(copy, act):
        def step(k, carry):
            act(copy(k))
            return carry

        lax.fori_loop(1, n, step, 0)

    def feat_step(k):
        def step(c, carry):
            cols = pl.ds(pl.multiple_of(c * chunk, chunk), chunk)
            ext[0:rows] = ds_ref[k, :, cols]
            ext[rows:] = jnp.where(last, 0.0, tail_in[k, :, cols].astype(f32))
            total = wt_ref[k, 0:1, cols] * ds_ref[k, :, cols]
            for lag in range(1, taps):
                total = total + wt_ref[k, lag : lag + 1, cols] * ext[lag : lag + rows]
            feat_out[k, :, cols] = total.astype(feat_out.dtype)
            return carry

        lax.fori_loop(0, width // chunk, step, 0)

    each(scatter, lambda c: c.start())
    sums[0] = part_ref[me]
    tail_hop.wait()
    feat_step(0)
    each(scatter, lambda c: c.wait())
    result = sums[0]
    for k in range(1, n):
        result = result + sums[k]
    gathered[me] = result
    each(gather, lambda c: c.start())
    feat_step(1)
    feat_step(2)
    each(gather, lambda c: c.wait())
    total_ref[...] = gathered[...]


def shards(features, out_grad, attn_parts, short_filt, med_filt, piece_home, piece_start):
    rows, width = out_grad.shape
    groups, taps = med_filt.shape
    short_taps = short_filt.shape[2]
    ctx_count = lax.axis_size("ctx")
    own_index = lax.axis_index("ctx")
    per_device = ctx_count // 2
    piece_rows = rows // per_device
    factor = 1.0 / math.sqrt(rows * ctx_count * GROUP)
    chunk = LANES if width % LANES == 0 else width
    f32, half = jnp.float32, features.dtype

    everyone = piece_home.reshape(ctx_count, per_device)
    positions = (piece_start // piece_rows).reshape(ctx_count, per_device)
    local_home = lax.dynamic_slice_in_dim(everyone, own_index, 1, 0)[0]
    device_ids = jnp.arange(ctx_count, dtype=jnp.int32)
    slot_ids = jnp.arange(per_device, dtype=jnp.int32)
    matches = local_home[None, :] == device_ids[:, None]
    send_slot = jnp.sum(jnp.where(matches, slot_ids[None, :], 0), axis=1)
    keyed = jnp.where(everyone == own_index, positions, -1)
    hits = jnp.any(keyed[:, :, None] == slot_ids[None, None, :], axis=1)
    source_of = jnp.sum(jnp.where(hits, device_ids[:, None], 0), axis=0)
    short_rows = jnp.transpose(short_filt, (0, 2, 1)).reshape(3 * short_taps, groups)
    filt = med_filt.astype(f32)
    filt_back = jnp.roll(filt[:, ::-1], 1, axis=1)
    tp_count = lax.axis_size("tp")
    blocks = 2 if rows % 32 == 0 else 1
    vmem = pl.BlockSpec(memory_space=pltpu.VMEM)
    smem = pl.BlockSpec(memory_space=pltpu.SMEM)
    dma = pltpu.SemaphoreType.DMA
    lanes = jax.ShapeDtypeStruct((rows, width), half)
    crossing = pltpu.VMEM((tp_count // 2, blocks, rows // blocks, width), half)
    flags = dma((tp_count // 2, blocks))
    routed = pltpu.VMEM((ctx_count, piece_rows, width), half)
    used = groups + 3 * short_taps
    share = -(-used // ctx_count)
    parts = (ctx_count, share, taps)
    held = pltpu.VMEM((rows, width), half)
    heads = pltpu.VMEM((3, 16, width), half)
    wide = pltpu.VMEM((3, rows, width), f32)
    peers = dma((ctx_count,))
    feat_grad, totals = pl.pallas_call(
        functools.partial(whole_kernel, ctx_count, tp_count),
        in_specs=[smem, smem] + [vmem] * 6,
        out_specs=(vmem, vmem),
        out_shape=(
            jax.ShapeDtypeStruct((3, rows, width), half),
            jax.ShapeDtypeStruct(parts, f32),
        ),
        scratch_shapes=[
            wide, held, held, heads, held, wide, held,
            pltpu.VMEM((3, short_taps, width), f32),
            pltpu.VMEM((groups, taps, 2 * taps), half),
            pltpu.VMEM((3 * short_taps, width), f32),
            pltpu.VMEM((ctx_count * share, taps), f32),
            pltpu.VMEM(parts, f32), pltpu.VMEM(parts, f32), pltpu.VMEM(parts, f32),
            heads, heads,
            crossing, crossing, crossing,
            pltpu.VMEM((rows, width), f32),
            pltpu.VMEM((per_device, piece_rows, width), f32),
            routed, routed,
            heads, held, held,
            pltpu.VMEM((rows + 16, chunk), f32),
            flags, flags, flags, flags,
            peers, peers, dma((4,)), dma((4,)),
            peers, peers, peers, peers,
        ],
        compiler_params=pltpu.CompilerParams(
            collective_id=0, has_side_effects=True, vmem_limit_bytes=48 * 1024 * 1024
        ),
        cost_estimate=cost(12 * groups * taps * taps * chunk, 40 * rows * width),
    )(
        send_slot.astype(jnp.int32), source_of.astype(jnp.int32), attn_parts[0], features,
        out_grad, short_rows, filt_back, filt,
    )
    flat_totals = totals.reshape(-1, taps)
    short_total = flat_totals[groups:used, :groups].reshape(3, short_taps, groups)
    return (
        feat_grad,
        jnp.transpose(short_total, (0, 2, 1)) * factor,
        flat_totals[:groups, ::-1] * factor,
    )


def solution(mesh):
    return jax.shard_map(
        shards,
        mesh=mesh,
        in_specs=(
            P(None, "ctx", "tp"),
            P("ctx", "tp"),
            P("tp", "ctx", None),
            P(None, "tp", None),
            P("tp", None),
            P(),
            P(),
        ),
        out_specs=(P(None, "ctx", "tp"), P(None, "tp", None), P("tp", None)),
        check_vma=False,
    )
```
